32 devices in a mesh: pair: 2 (over y), src: 8 (over z, x), tgt: 2 (over core).
Axes of the slice: x: 2, y: 2, z: 4, core: 2. Of those that a mesh axis runs over, the one named last changes fastest.
Arguments:
- source_features: bfloat16 [64, 8, 256], P('pair', 'src'), parts along dimension 0, may hold values from -6 to 6
- target_features: bfloat16 [128, 8, 256], P(('pair', 'tgt'), 'src'), parts along dimension 0, may hold values from -6 to 6
- source_rows: int32 [8], P('pair'), parts along dimension 0, may hold values from 0 to 31
- target_cols: int32 [16], P('pair'), parts along dimension 0, may hold values from 0 to 7, each once
- target_kernel_one: bfloat16 [3, 3, 16, 16], replicated, may hold values from -0.75 to 0.75
- source_kernel: bfloat16 [3, 3, 16, 16], replicated, may hold values from -0.75 to 0.75
- target_kernel_two: bfloat16 [3, 3, 16, 16], replicated, may hold values from -0.75 to 0.75
Outputs:
- filtered: bfloat16 [8, 8, 64, 128], P('pair', 'src', 'tgt'), parts along dimension 0
The draws below stay inside these ranges and needn't reach their ends.
There are 2 independent parts, one for each index of `pair`. The reference program is written for one: setup_inputs(seed, part) draws one part's arguments, and reference() takes and returns one part's arrays. A program takes and returns all parts, laid end to end along the dimension named above; an argument that names none is the same for every part. Nothing has to cross between parts.
Inputs may be any that keep to these rules, and one draw needn't show every extreme that they name: `target_cols`: each column index appears once.
All inputs are finite; a program needn't handle non-finite values.
Results may differ from the reference program's by a relative error of at most 0.0074.
Values may be sent and summed in bfloat16 or wider, within the bound.
No kernel may reach another device: no remote copies, remote signals or barrier semaphores. Data moves between devices by JAX's collectives and lax.ppermute only.
A program may use at most 128 MiB of HBM per device.

```python
import jax
import jax.numpy as jnp
from jax import lax

HS_MAP = 32
HS = 4
HT = 64
F = 256
G = 16
WS = 8
WT = 8


def place_ends(drawn, stream_key, smallest, high):
    place = [jax.random.randint(jax.random.fold_in(stream_key, axis), (), 0, length) for axis, length in enumerate(drawn.shape)]
    widest = drawn.shape.index(max(drawn.shape))
    beside = place[:widest] + [(place[widest] + 1) % drawn.shape[widest]] + place[widest + 1:]
    return drawn.at[tuple(place)].set(smallest).at[tuple(beside)].set(high)


def level_of(rng, dims, cuts, least, high):
    loudness = 1.0
    for position, parts in cuts:
        steps = jax.random.uniform(jax.random.fold_in(jax.random.fold_in(rng, 6), position), (parts,), jnp.float32, least / len(cuts), high / len(cuts))
        loudness = loudness * jnp.repeat(jnp.exp(steps), dims[position] // parts).reshape((-1,) + (1,) * (len(dims) - 1 - position))
    return loudness


def bell_draw(own_key, shape, width, reach, pieces=(), held_as=jnp.bfloat16):
    entries = width * jax.random.normal(own_key, shape, jnp.float32)
    if pieces:
        entries = entries * level_of(own_key, shape, pieces, -0.22, 0.18)
    return jnp.clip(entries, -reach, reach).astype(held_as)


def setup_inputs(seed: int = 0, part: int = 0) -> dict:
    seeds = jax.random.split(jax.random.key(seed), 8)
    part_splits = jax.random.split(jax.random.fold_in(seeds[7], part), 8)
    source_features = bell_draw(part_splits[0], (HS_MAP, WS, F), 1.0, 6.0, ((1, 8),))
    target_features = bell_draw(part_splits[1], (HT, WT, F), 1.0, 6.0, ((0, 2), (1, 8)))
    source_rows = place_ends(jax.random.randint(part_splits[2], (HS,), 0, HS_MAP), jax.random.fold_in(part_splits[2], 1), 0, HS_MAP - 1).astype(jnp.int32)
    target_cols = jax.random.permutation(part_splits[3], WT).astype(jnp.int32)
    target_kernel_one = bell_draw(seeds[4], (3, 3, G, G), (9 * G // 2) ** -0.5, 0.75)
    source_kernel = bell_draw(seeds[5], (3, 3, G, G), (9 * G // 2) ** -0.5, 0.75)
    target_kernel_two = bell_draw(seeds[6], (3, 3, G, G), (9 * G // 2) ** -0.5, 0.75)
    return dict(source_features=source_features, target_features=target_features, source_rows=source_rows, target_cols=target_cols, target_kernel_one=target_kernel_one, source_kernel=source_kernel, target_kernel_two=target_kernel_two)


def plane_filter(plane_slice, kernel):
    height = plane_slice.shape[0]
    breadth = plane_slice.shape[1]
    padded = jnp.pad(plane_slice, ((1, 1), (1, 1), (0, 0)))
    running = jnp.zeros((height, breadth, kernel.shape[3]), jnp.float32)
    for offset_y in range(3):
        for offset_x in range(3):
            running = running + jnp.einsum('abi,io->abo', padded[offset_y:offset_y + height, offset_x:offset_x + breadth], kernel[offset_y, offset_x], precision=lax.Precision.HIGHEST)
    return jnp.maximum(running, 0.0).astype(jnp.bfloat16)


def target_section(volume, kernel):
    groups = volume.shape[4]
    flattened = volume.reshape(HS * WS, HT, WT, groups)
    result = lax.map(lambda plane_slice: plane_filter(plane_slice.astype(jnp.float32), kernel), flattened)
    return result.reshape(HS, WS, HT, WT, groups)


def source_section(volume, kernel):
    groups = volume.shape[4]
    reordered = volume.transpose(2, 3, 0, 1, 4).reshape(HT * WT, HS, WS, groups)
    result = lax.map(lambda plane_slice: plane_filter(plane_slice.astype(jnp.float32), kernel), reordered)
    return result.reshape(HT, WT, HS, WS, groups).transpose(2, 3, 0, 1, 4)


def reference(source_features, target_features, source_rows, target_cols, target_kernel_one, source_kernel, target_kernel_two):
    groups = target_kernel_one.shape[2]
    channels = source_features.shape[2] // groups
    src_window = jnp.take(source_features, source_rows.astype(jnp.int32), axis=0)
    tgt_window = jnp.take(target_features, target_cols.astype(jnp.int32), axis=1)
    source_grouped = src_window.astype(jnp.float32).reshape(HS, WS, groups, channels)
    target_grouped = tgt_window.astype(jnp.float32).reshape(HT, WT, groups, channels)
    volume = jnp.einsum('hsgc,rwgc->hsrwg', source_grouped, target_grouped, precision=lax.Precision.HIGHEST)
    volume = (volume * (channels ** -0.5)).astype(jnp.bfloat16)
    section_one = target_section(volume, target_kernel_one.astype(jnp.float32))
    section_two = source_section(section_one, source_kernel.astype(jnp.float32))
    section_three = target_section(section_two, target_kernel_two.astype(jnp.float32))
    return section_three.reshape(HS, WS, HT, WT * groups)
```

```python
import functools
import math

import jax
import jax.numpy as jnp
from jax import lax
from jax.experimental import pallas as pl
from jax.experimental.pallas import tpu as pltpu
from jax.sharding import PartitionSpec as P

LANES = 128
TILE = 8


def offset_of(entry, bits):
    return sum(((entry >> b) & 1) << (bits - 1 - b) for b in range(bits))


def entry_of(offset, bits):
    entry = 0
    for b in range(bits):
        entry = entry + (((offset >> b) & 1) << (bits - 1 - b))
    return entry


def pack_kernel(rows_ref, source_ref, target_ref, out_ref, wide_ref):
    rows = target_ref.shape[0]
    window = rows_ref.shape[0]
    out_ref[0, :rows, :] = target_ref[...]
    wide_ref[...] = source_ref[...].astype(jnp.float32)
    lines = [wide_ref[pl.ds(rows_ref[h], 1), :] for h in range(window)]
    blank = out_ref.shape[1] - rows - window
    if blank:
        lines.append(jnp.zeros((blank, wide_ref.shape[1]), jnp.float32))
    out_ref[0, rows:, :] = jnp.concatenate(lines, axis=0).astype(out_ref.dtype)


def pack(source_rows, source, target, height):
    return pl.pallas_call(
        pack_kernel,
        out_shape=jax.ShapeDtypeStruct((1, height, target.shape[1]), target.dtype),
        in_specs=[
            pl.BlockSpec(memory_space=pltpu.SMEM),
            pl.BlockSpec(memory_space=pltpu.VMEM),
            pl.BlockSpec(memory_space=pltpu.VMEM),
        ],
        out_specs=pl.BlockSpec(memory_space=pltpu.VMEM),
        scratch_shapes=[pltpu.VMEM(source.shape, jnp.float32)],
        name="pack",
    )(source_rows, source, target)


def widen(block):
    return jnp.concatenate(
        [
            block.astype(jnp.float32),
            jnp.zeros((block.shape[0], LANES - block.shape[1]), jnp.float32),
        ],
        axis=1,
    )


def band_rows(kernel_ref, a, place, breadth):
    groups = kernel_ref.shape[2]
    total = jnp.zeros((groups, LANES), jnp.float32)
    for b in range(3):
        out_place = place - b + 1
        if 0 <= out_place < breadth:
            piece = widen(kernel_ref[a, b])
            total = total + (pltpu.roll(piece, out_place * groups, 1) if out_place else piece)
    return total


def weights_kernel(bits, cols_ref, one_ref, source_ref, two_ref, band_one, blocks, band_two):
    groups = one_ref.shape[2]
    breadth = LANES // groups
    here = lax.axis_index("src")
    for place in range(breadth):
        entry = entry_of(jnp.bitwise_xor(cols_ref[place], here), bits)
        start = pl.multiple_of(entry * groups, groups)
        for a in range(3):
            lanes = slice(a * LANES, (a + 1) * LANES)
            band_one[pl.ds(start, groups), lanes] = band_rows(one_ref, a, place, breadth).astype(
                band_one.dtype
            )
            band_two[place * groups : (place + 1) * groups, lanes] = band_rows(
                two_ref, a, place, breadth
            ).astype(band_two.dtype)
            for b in range(3):
                piece = widen(source_ref[a, b])
                piece = pltpu.roll(piece, place * groups, 1) if place else piece
                row = b * LANES + place * groups
                blocks[row : row + groups, lanes] = piece.astype(blocks.dtype)


def weights(target_cols, one, source, two, bits):
    smem = pl.BlockSpec(memory_space=pltpu.SMEM)
    vmem = pl.BlockSpec(memory_space=pltpu.VMEM)
    return pl.pallas_call(
        functools.partial(weights_kernel, bits),
        out_shape=[
            jax.ShapeDtypeStruct((LANES, 3 * LANES), one.dtype),
            jax.ShapeDtypeStruct((3 * LANES, 3 * LANES), one.dtype),
            jax.ShapeDtypeStruct((LANES, 3 * LANES), one.dtype),
        ],
        in_specs=[smem, vmem, vmem, vmem],
        out_specs=[vmem, vmem, vmem],
        name="weights",
    )(target_cols, one, source, two)


def shifted_sum(product):
    rows = product.shape[1]
    below = pltpu.roll(product[:, :, :LANES], 1, 1)
    above = pltpu.roll(product[:, :, 2 * LANES :], rows - 1, 1)
    return below + product[:, :, LANES : 2 * LANES] + above


def swap_lane_groups(arrays, groups):
    lane_group = lax.broadcasted_iota(jnp.int32, arrays[0].shape, 1) // groups
    count = LANES // groups
    bit = count // 2
    while bit:
        lower = (lane_group // bit) % 2 == 0
        result = list(arrays)
        for index in range(len(arrays)):
            if index & bit:
                continue
            low, high = arrays[index], arrays[index | bit]
            result[index] = jnp.where(lower, low, pltpu.roll(high, bit * groups, 1))
            result[index | bit] = jnp.where(lower, pltpu.roll(low, LANES - bit * groups, 1), high)
        arrays = result
        bit //= 2
    return arrays


def filter_kernel(
    bits,
    groups,
    window,
    near_a,
    near_b,
    far_a,
    far_b,
    band_one,
    blocks,
    band_two,
    out_ref,
):
    count = 1 << bits
    half = count // 2
    rows = out_ref.shape[1]
    high = rows + TILE
    width = near_a.shape[2]
    channels = width // groups
    here = lax.axis_index("src")
    first = lax.axis_index("tgt") == 0

    def near(entry):
        return near_a.at[entry] if entry < half else near_b.at[entry - half]

    def far(entry):
        return far_a.at[entry] if entry < half else far_b.at[entry - half]

    def source_rows(entry):
        return near(entry)[rows : rows + TILE, :].astype(jnp.float32)

    before = jnp.zeros((TILE, width), jnp.float32)
    after = jnp.zeros((TILE, width), jnp.float32)
    for bit in range(bits):
        offset = (2 << bit) - 1
        candidate = source_rows(entry_of(offset, bits))
        before = jnp.where(jnp.bitwise_xor(here, here - 1) == offset, candidate, before)
        after = jnp.where(jnp.bitwise_xor(here, here + 1) == offset, candidate, after)
    row_group = lax.broadcasted_iota(jnp.int32, (groups, width), 0)
    own_group = row_group == lax.broadcasted_iota(jnp.int32, (groups, width), 1) // channels
    spread = []
    for part in (before, source_rows(0), after):
        for h in range(window):
            line = jnp.broadcast_to(part[h : h + 1, :], (groups, width))
            spread.append(jnp.where(own_group, line, 0.0))
    spread = jnp.concatenate(spread, axis=0).astype(jnp.bfloat16)

    base, edge = [], []
    for entry in range(count):
        even = bin(entry).count("1") % 2 == 0
        mine, other = (near(entry), far(entry)) if even else (far(entry), near(entry))
        base.append(mine[:rows, :])
        edge.append(
            jnp.where(
                first,
                other[:TILE, :].astype(jnp.float32),
                other[rows - TILE : rows, :].astype(jnp.float32),
            )
        )
    contract = (((1,), (1,)), ((), ()))
    base = lax.dot_general(
        jnp.concatenate(base, axis=0), spread, contract, preferred_element_type=jnp.float32
    )
    edge = lax.dot_general(
        jnp.concatenate(edge, axis=0).astype(jnp.bfloat16),
        spread,
        contract,
        preferred_element_type=jnp.float32,
    )
    outside_from = jnp.where(first, high - 2, rows)

    def keep_inside(value, axis):
        row = lax.broadcasted_iota(jnp.int32, value.shape, axis)
        return jnp.where((row >= outside_from) & (row < outside_from + 2), 0.0, value)

    per_tile = LANES // groups
    planes = []
    for tile in range(-(-3 * window // per_tile)):
        lanes = slice(tile * LANES, min((tile + 1) * LANES, 3 * window * groups))
        stack = []
        for entry in range(count):
            block = jnp.concatenate(
                [
                    base[entry * rows : (entry + 1) * rows, lanes],
                    edge[entry * TILE : (entry + 1) * TILE, lanes],
                ],
                axis=0,
            )
            missing = LANES - block.shape[1]
            if missing:
                block = jnp.concatenate([block, jnp.zeros((high, missing), jnp.float32)], axis=1)
            stack.append(block)
        planes += swap_lane_groups(stack, groups)
    planes = [
        keep_inside(plane * channels ** (-0.5), 0) for plane in planes[: 3 * window]
    ]
    volume = jnp.concatenate(planes, axis=0).astype(jnp.bfloat16)

    product = jnp.dot(volume, band_one[...], preferred_element_type=jnp.float32)
    one = shifted_sum(product.reshape(3 * window, high, 3 * LANES))
    one = keep_inside(jnp.maximum(one, 0.0), 1)
    one = one.reshape(3, window * high, LANES).astype(jnp.bfloat16)
    product = jnp.dot(
        jnp.concatenate([one[0], one[1], one[2]], axis=1),
        blocks[...],
        preferred_element_type=jnp.float32,
    )
    product = product.reshape(window, high, 3 * LANES)
    two = []
    for h in range(window):
        total = product[h, :, LANES : 2 * LANES]
        if h > 0:
            total = total + product[h - 1, :, :LANES]
        if h < window - 1:
            total = total + product[h + 1, :, 2 * LANES :]
        two.append(jnp.maximum(total, 0.0))
    two = jnp.concatenate(two, axis=0).astype(jnp.bfloat16)
    product = jnp.dot(two, band_two[...], preferred_element_type=jnp.float32)
    three = shifted_sum(product.reshape(window, high, 3 * LANES))
    out_ref[...] = jnp.maximum(three[:, :rows, :], 0.0).astype(out_ref.dtype)


def filter_all(entries, matrices, bits, groups, window, rows):
    vmem = pl.BlockSpec(memory_space=pltpu.VMEM)
    return pl.pallas_call(
        functools.partial(filter_kernel, bits, groups, window),
        out_shape=jax.ShapeDtypeStruct((window, rows, LANES), jnp.bfloat16),
        in_specs=[vmem] * 7,
        out_specs=vmem,
        name="filter",
    )(*entries, *matrices)


def fast_local(
    source_features,
    target_features,
    source_rows,
    target_cols,
    target_kernel_one,
    source_kernel,
    target_kernel_two,
):
    groups = source_kernel.shape[2]
    window = source_rows.shape[0]
    rows = target_features.shape[0]
    count = lax.axis_size("src")
    bits = count.bit_length() - 1
    height = rows + -(-window // TILE) * TILE
    held = pack(source_rows, source_features[:, 0], target_features[:, 0], height)
    recent = None
    for b in range(bits):
        if recent is not None:
            held = jnp.concatenate([held, recent], axis=0)
        mask = count >> (b + 1)
        pairs = [
            (2 * s + t, 2 * (s ^ mask) + 1 - t) for s in range(count) for t in range(2)
        ]
        recent = lax.ppermute(held, ("src", "tgt"), pairs)
    other = [(0, 1), (1, 0)]
    entries = (held, recent, lax.ppermute(held, "tgt", other), lax.ppermute(recent, "tgt", other))
    matrices = weights(target_cols, target_kernel_one, source_kernel, target_kernel_two, bits)
    return filter_all(entries, matrices, bits, groups, window, rows)[:, None]


def with_halo(block, sides, width):
    for axis, dim in sides:
        count = lax.axis_size(axis)
        forward = [(i, i + 1) for i in range(count - 1)]
        backward = [(target, source) for source, target in forward]
        low = lax.ppermute(
            lax.slice_in_dim(block, block.shape[dim] - width, None, axis=dim), axis, forward
        )
        high = lax.ppermute(lax.slice_in_dim(block, 0, width, axis=dim), axis, backward)
        block = jnp.concatenate([low, block, high], axis=dim)
    return block


def build_toeplitz(kernel, breadth):
    groups = kernel.shape[2]
    span_width = breadth * groups
    row_index = lax.broadcasted_iota(jnp.int32, (3, breadth, breadth), 1)
    col_index = lax.broadcasted_iota(jnp.int32, (3, breadth, breadth), 2)
    tap_index = lax.broadcasted_iota(jnp.int32, (3, breadth, breadth), 0)
    shifts = (row_index - col_index == tap_index - 1).astype(jnp.bfloat16)
    matrices = []
    for offset_y in range(3):
        banded = jnp.einsum(
            "xab,xio->aibo", shifts, kernel[offset_y], preferred_element_type=jnp.float32
        )
        matrices.append(banded.astype(jnp.bfloat16).reshape(span_width, span_width))
    return jnp.stack(matrices)


def banded_pass(slices, matrices):
    span_width = matrices.shape[1]
    running = jnp.dot(
        slices[0].reshape(-1, span_width), matrices[0], preferred_element_type=jnp.float32
    )
    for offset in range(1, 3):
        running = running + jnp.dot(
            slices[offset].reshape(-1, span_width),
            matrices[offset],
            preferred_element_type=jnp.float32,
        )
    return jnp.maximum(running, 0.0).astype(jnp.bfloat16).reshape(slices[0].shape)


def target_pass(padded, matrices):
    row_count = padded.shape[1] - 2
    return banded_pass([padded[:, offset : offset + row_count] for offset in range(3)], matrices)


def column_filter(neighbours, source_kernel, groups, window_rows):
    bordered = jnp.pad(neighbours, ((0, 0), (1, 1), (0, 0), (0, 0)))
    span_width = neighbours.shape[3]
    repeats = math.gcd(span_width // groups, max(1, 128 // groups))
    block_width = repeats * groups
    diagonal = jnp.einsum(
        "ab,yxij->yxaibj", jnp.eye(repeats, dtype=jnp.float32), source_kernel.astype(jnp.float32)
    )
    diagonal = diagonal.reshape(3, 3, block_width, block_width).astype(jnp.bfloat16)
    running = jnp.zeros((neighbours[1].size // block_width, block_width), jnp.float32)
    for offset in range(3):
        window = bordered[:, offset : offset + window_rows].reshape(3, -1, block_width)
        running = running + jnp.einsum(
            "xmc,xcd->md", window, diagonal[offset], preferred_element_type=jnp.float32
        )
    return jnp.maximum(running, 0.0).astype(jnp.bfloat16).reshape(neighbours[1].shape)


def local(
    source_features,
    target_features,
    source_rows,
    target_cols,
    target_kernel_one,
    source_kernel,
    target_kernel_two,
):
    groups = source_kernel.shape[2]
    channels = source_features.shape[2] // groups
    window_rows = source_rows.shape[0]
    selected = jnp.take(source_features[:, 0], source_rows, axis=0)
    columns = selected[None]
    column_count = columns.shape[0]
    columns = columns.reshape(column_count, window_rows, groups, channels)
    gathered = lax.all_gather(target_features, "src", axis=1, tiled=True)
    gathered = jnp.take(gathered, target_cols, axis=1)
    target_rows = gathered.shape[0]
    breadth = gathered.shape[1]
    grouped = gathered.reshape(target_rows, breadth, groups, channels)
    volume = jnp.einsum("khgc,rwgc->khrwg", columns, grouped, preferred_element_type=jnp.float32)
    volume = (
        (volume * channels ** (-0.5))
        .astype(jnp.bfloat16)
        .reshape(column_count * window_rows, target_rows, breadth * groups)
    )
    padded = with_halo(volume, (("tgt", 1),), 1)
    filtered_one = target_pass(padded, build_toeplitz(target_kernel_one, breadth))
    neighbours = with_halo(filtered_one[None], (("src", 0),), 1)
    filtered_two = column_filter(neighbours, source_kernel, groups, window_rows)
    padded_last = with_halo(filtered_two, (("tgt", 1),), 1)
    filtered_three = target_pass(padded_last, build_toeplitz(target_kernel_two, breadth))
    return filtered_three[:, None]


def solution(mesh):
    def step(*args):
        source, target, source_rows, cols, _, source_kernel, _ = args
        count = lax.axis_size("src")
        fits = (
            lax.axis_size("tgt") == 2
            and count > 1
            and count & (count - 1) == 0
            and source.shape[1] == 1
            and target.shape[1] == 1
            and cols.shape[0] == count
            and count * source_kernel.shape[2] == LANES
            and source_rows.shape[0] <= TILE
            and target.shape[0] % (2 * TILE) == 0
        )
        return (fast_local if fits else local)(*args)

    return jax.shard_map(
        step,
        mesh=mesh,
        in_specs=(
            P("pair", "src", None),
            P(("pair", "tgt"), "src", None),
            P("pair"),
            P("pair"),
            P(),
            P(),
            P(),
        ),
        out_specs=P("pair", "src", "tgt", None),
        check_vma=False,
    )
```

```python
import functools
import math

import jax
import jax.numpy as jnp
from jax import lax
from jax.experimental import pallas as pl
from jax.experimental.pallas import tpu as pltpu
from jax.sharding import PartitionSpec as P

LANES = 128
TILE = 8


def rounds_of(count):
    rounds = []
    while count > 4:
        count //= 2
        rounds.append([count])
    rounds.append(list(range(1, count)))
    return rounds


def entries_of(count):
    entries = [(0, 0)]
    for masks in rounds_of(count):
        entries = entries + [
            (offset ^ mask, hops + 1) for mask in masks for offset, hops in entries
        ]
    return entries


def pack_kernel(rows_hbm, source_hbm, target_hbm, out_ref, rows_ref, source_ref, wide_ref, sems):
    rows = target_hbm.shape[0]
    window = rows_hbm.shape[0]
    copies = [
        pltpu.make_async_copy(rows_hbm, rows_ref, sems.at[0]),
        pltpu.make_async_copy(source_hbm, source_ref, sems.at[1]),
        pltpu.make_async_copy(target_hbm, out_ref.at[0, pl.ds(0, rows)], sems.at[2]),
    ]
    for copy in copies:
        copy.start()
    copies[1].wait()
    wide_ref[...] = source_ref[...].astype(jnp.float32)
    copies[0].wait()
    lines = [wide_ref[pl.ds(rows_ref[h], 1), :] for h in range(window)]
    blank = out_ref.shape[1] - rows - window
    if blank:
        lines.append(jnp.zeros((blank, wide_ref.shape[1]), jnp.float32))
    out_ref[0, rows:, :] = jnp.concatenate(lines, axis=0).astype(out_ref.dtype)
    copies[2].wait()


def pack(source_rows, source, target, height):
    return pl.pallas_call(
        pack_kernel,
        out_shape=jax.ShapeDtypeStruct((1, height, target.shape[1]), target.dtype),
        in_specs=[pl.BlockSpec(memory_space=pltpu.HBM)] * 3,
        out_specs=pl.BlockSpec(memory_space=pltpu.VMEM),
        scratch_shapes=[
            pltpu.SMEM(source_rows.shape, source_rows.dtype),
            pltpu.VMEM(source.shape, source.dtype),
            pltpu.VMEM(source.shape, jnp.float32),
            pltpu.SemaphoreType.DMA((3,)),
        ],
        compiler_params=pltpu.CompilerParams(vmem_limit_bytes=4 << 20),
        name="pack",
    )(*(pltpu.with_memory_space_constraint(x, pltpu.HBM) for x in (source_rows, source, target)))


def widen(block):
    return jnp.concatenate(
        [
            block.astype(jnp.float32),
            jnp.zeros((block.shape[0], LANES - block.shape[1]), jnp.float32),
        ],
        axis=1,
    )


def band_rows(kernel_ref, a, place, breadth):
    groups = kernel_ref.shape[2]
    total = jnp.zeros((groups, LANES), jnp.float32)
    for b in range(3):
        out_place = place - b + 1
        if 0 <= out_place < breadth:
            piece = widen(kernel_ref[a, b])
            total = total + (pltpu.roll(piece, out_place * groups, 1) if out_place else piece)
    return total


def weights_kernel(offsets, cols_ref, one_ref, source_ref, two_ref, band_one, blocks, band_two):
    groups = one_ref.shape[2]
    breadth = LANES // groups
    here = lax.axis_index("src")
    for place in range(breadth):
        offset = jnp.bitwise_xor(cols_ref[place], here)
        entry = sum(jnp.where(offset == value, index, 0) for index, value in enumerate(offsets))
        start = pl.multiple_of(entry * groups, groups)
        for a in range(3):
            lanes = slice(a * LANES, (a + 1) * LANES)
            band_one[pl.ds(start, groups), lanes] = band_rows(one_ref, a, place, breadth).astype(
                band_one.dtype
            )
            band_two[place * groups : (place + 1) * groups, lanes] = band_rows(
                two_ref, a, place, breadth
            ).astype(band_two.dtype)
            for b in range(3):
                piece = widen(source_ref[a, b])
                piece = pltpu.roll(piece, place * groups, 1) if place else piece
                row = b * LANES + place * groups
                blocks[row : row + groups, lanes] = piece.astype(blocks.dtype)


def weights(target_cols, one, source, two, offsets):
    smem = pl.BlockSpec(memory_space=pltpu.SMEM)
    vmem = pl.BlockSpec(memory_space=pltpu.VMEM)
    return pl.pallas_call(
        functools.partial(weights_kernel, offsets),
        out_shape=[
            jax.ShapeDtypeStruct((LANES, 3 * LANES), one.dtype),
            jax.ShapeDtypeStruct((3 * LANES, 3 * LANES), one.dtype),
            jax.ShapeDtypeStruct((LANES, 3 * LANES), one.dtype),
        ],
        in_specs=[smem, vmem, vmem, vmem],
        out_specs=[vmem, vmem, vmem],
        compiler_params=pltpu.CompilerParams(vmem_limit_bytes=4 << 20),
        name="weights",
    )(target_cols, one, source, two)


def shifted_sum(product):
    rows = product.shape[1]
    below = pltpu.roll(product[:, :, :LANES], 1, 1)
    above = pltpu.roll(product[:, :, 2 * LANES :], rows - 1, 1)
    return below + product[:, :, LANES : 2 * LANES] + above


def swap_lane_groups(arrays, groups):
    lane_group = lax.broadcasted_iota(jnp.int32, arrays[0].shape, 1) // groups
    count = LANES // groups
    bit = count // 2
    while bit:
        lower = (lane_group // bit) % 2 == 0
        result = list(arrays)
        for index in range(len(arrays)):
            if index & bit:
                continue
            low, high = arrays[index], arrays[index | bit]
            result[index] = jnp.where(lower, low, pltpu.roll(high, bit * groups, 1))
            result[index | bit] = jnp.where(lower, pltpu.roll(low, LANES - bit * groups, 1), high)
        arrays = result
        bit //= 2
    return arrays


def filter_kernel(entries, groups, window, *refs):
    *parts, band_one, blocks, band_two, out_ref = refs
    count = len(entries)
    rows = out_ref.shape[1]
    high = rows + TILE
    width = parts[0].shape[2]
    channels = width // groups
    here = lax.axis_index("src")
    first = lax.axis_index("tgt") == 0
    near = [part.at[k] for part in parts[: len(parts) // 2] for k in range(part.shape[0])]
    far = [part.at[k] for part in parts[len(parts) // 2 :] for k in range(part.shape[0])]
    offsets = [offset for offset, _ in entries]

    def source_rows(entry):
        return near[entry][rows : rows + TILE, :].astype(jnp.float32)

    before = jnp.zeros((TILE, width), jnp.float32)
    after = jnp.zeros((TILE, width), jnp.float32)
    for bit in range(count.bit_length() - 1):
        offset = (2 << bit) - 1
        candidate = source_rows(offsets.index(offset))
        before = jnp.where(jnp.bitwise_xor(here, here - 1) == offset, candidate, before)
        after = jnp.where(jnp.bitwise_xor(here, here + 1) == offset, candidate, after)
    row_group = lax.broadcasted_iota(jnp.int32, (groups, width), 0)
    own_group = row_group == lax.broadcasted_iota(jnp.int32, (groups, width), 1) // channels
    spread = []
    for part in (before, source_rows(0), after):
        for h in range(window):
            line = jnp.broadcast_to(part[h : h + 1, :], (groups, width))
            spread.append(jnp.where(own_group, line, 0.0))
    spread = jnp.concatenate(spread, axis=0).astype(jnp.bfloat16)

    base, edge = [], []
    for entry in range(count):
        mine, other = near[entry], far[entry]
        if entries[entry][1] % 2:
            mine, other = other, mine
        base.append(mine[:rows, :])
        edge.append(
            jnp.where(
                first,
                other[:TILE, :].astype(jnp.float32),
                other[rows - TILE : rows, :].astype(jnp.float32),
            )
        )
    contract = (((1,), (1,)), ((), ()))
    base = lax.dot_general(
        jnp.concatenate(base, axis=0), spread, contract, preferred_element_type=jnp.float32
    )
    edge = lax.dot_general(
        jnp.concatenate(edge, axis=0).astype(jnp.bfloat16),
        spread,
        contract,
        preferred_element_type=jnp.float32,
    )
    outside_from = jnp.where(first, high - 2, rows)

    def keep_inside(value, axis):
        row = lax.broadcasted_iota(jnp.int32, value.shape, axis)
        return jnp.where((row >= outside_from) & (row < outside_from + 2), 0.0, value)

    per_tile = LANES // groups
    planes = []
    for tile in range(-(-3 * window // per_tile)):
        lanes = slice(tile * LANES, min((tile + 1) * LANES, 3 * window * groups))
        stack = []
        for entry in range(count):
            block = jnp.concatenate(
                [
                    base[entry * rows : (entry + 1) * rows, lanes],
                    edge[entry * TILE : (entry + 1) * TILE, lanes],
                ],
                axis=0,
            )
            missing = LANES - block.shape[1]
            if missing:
                block = jnp.concatenate([block, jnp.zeros((high, missing), jnp.float32)], axis=1)
            stack.append(block)
        planes += swap_lane_groups(stack, groups)
    planes = [
        keep_inside(plane * channels ** (-0.5), 0) for plane in planes[: 3 * window]
    ]
    volume = jnp.concatenate(planes, axis=0).astype(jnp.bfloat16)

    product = jnp.dot(volume, band_one[...], preferred_element_type=jnp.float32)
    one = shifted_sum(product.reshape(3 * window, high, 3 * LANES))
    one = keep_inside(jnp.maximum(one, 0.0), 1)
    one = one.reshape(3, window * high, LANES).astype(jnp.bfloat16)
    product = jnp.dot(
        jnp.concatenate([one[0], one[1], one[2]], axis=1),
        blocks[...],
        preferred_element_type=jnp.float32,
    )
    product = product.reshape(window, high, 3 * LANES)
    two = []
    for h in range(window):
        total = product[h, :, LANES : 2 * LANES]
        if h > 0:
            total = total + product[h - 1, :, :LANES]
        if h < window - 1:
            total = total + product[h + 1, :, 2 * LANES :]
        two.append(jnp.maximum(total, 0.0))
    two = jnp.concatenate(two, axis=0).astype(jnp.bfloat16)
    product = jnp.dot(two, band_two[...], preferred_element_type=jnp.float32)
    three = shifted_sum(product.reshape(window, high, 3 * LANES))
    out_ref[...] = jnp.maximum(three[:, :rows, :], 0.0).astype(out_ref.dtype)


def filter_all(parts, matrices, entries, groups, window, rows):
    vmem = pl.BlockSpec(memory_space=pltpu.VMEM)
    return pl.pallas_call(
        functools.partial(filter_kernel, entries, groups, window),
        out_shape=jax.ShapeDtypeStruct((window, rows, LANES), jnp.bfloat16),
        in_specs=[vmem] * (len(parts) + len(matrices)),
        out_specs=vmem,
        compiler_params=pltpu.CompilerParams(vmem_limit_bytes=8 << 20),
        name="filter",
    )(*parts, *matrices)


def fast_local(
    source_features,
    target_features,
    source_rows,
    target_cols,
    target_kernel_one,
    source_kernel,
    target_kernel_two,
):
    groups = source_kernel.shape[2]
    window = source_rows.shape[0]
    rows = target_features.shape[0]
    count = lax.axis_size("src")
    entries = entries_of(count)
    height = rows + -(-window // TILE) * TILE
    held = pack(source_rows, source_features[:, 0], target_features[:, 0], height)
    source_rounds = rounds_of(count)
    matrices = None
    for masks in source_rounds:
        arrived = []
        for mask in masks:
            pairs = [
                (2 * s + t, 2 * (s ^ mask) + 1 - t) for s in range(count) for t in range(2)
            ]
            arrived.append(lax.ppermute(held, ("src", "tgt"), pairs))
        if matrices is None:
            held, target_cols = lax.optimization_barrier((held, target_cols))
            matrices = weights(
                target_cols,
                target_kernel_one,
                source_kernel,
                target_kernel_two,
                [offset for offset, _ in entries],
            )
            arrived, matrices = lax.optimization_barrier((arrived, matrices))
        if masks is not source_rounds[-1]:
            held = jnp.concatenate([held, *arrived], axis=0)
    near = [held, *arrived]
    far = [lax.ppermute(part, "tgt", [(0, 1), (1, 0)]) for part in near]
    return filter_all(near + far, matrices, entries, groups, window, rows)[:, None]


def with_halo(block, sides, width):
    for axis, dim in sides:
        count = lax.axis_size(axis)
        forward = [(i, i + 1) for i in range(count - 1)]
        backward = [(target, source) for source, target in forward]
        low = lax.ppermute(
            lax.slice_in_dim(block, block.shape[dim] - width, None, axis=dim), axis, forward
        )
        high = lax.ppermute(lax.slice_in_dim(block, 0, width, axis=dim), axis, backward)
        block = jnp.concatenate([low, block, high], axis=dim)
    return block


def build_toeplitz(kernel, breadth):
    groups = kernel.shape[2]
    span_width = breadth * groups
    row_index = lax.broadcasted_iota(jnp.int32, (3, breadth, breadth), 1)
    col_index = lax.broadcasted_iota(jnp.int32, (3, breadth, breadth), 2)
    tap_index = lax.broadcasted_iota(jnp.int32, (3, breadth, breadth), 0)
    shifts = (row_index - col_index == tap_index - 1).astype(jnp.bfloat16)
    matrices = []
    for offset_y in range(3):
        banded = jnp.einsum(
            "xab,xio->aibo", shifts, kernel[offset_y], preferred_element_type=jnp.float32
        )
        matrices.append(banded.astype(jnp.bfloat16).reshape(span_width, span_width))
    return jnp.stack(matrices)


def banded_pass(slices, matrices):
    span_width = matrices.shape[1]
    running = jnp.dot(
        slices[0].reshape(-1, span_width), matrices[0], preferred_element_type=jnp.float32
    )
    for offset in range(1, 3):
        running = running + jnp.dot(
            slices[offset].reshape(-1, span_width),
            matrices[offset],
            preferred_element_type=jnp.float32,
        )
    return jnp.maximum(running, 0.0).astype(jnp.bfloat16).reshape(slices[0].shape)


def target_pass(padded, matrices):
    row_count = padded.shape[1] - 2
    return banded_pass([padded[:, offset : offset + row_count] for offset in range(3)], matrices)


def column_filter(neighbours, source_kernel, groups, window_rows):
    bordered = jnp.pad(neighbours, ((0, 0), (1, 1), (0, 0), (0, 0)))
    span_width = neighbours.shape[3]
    repeats = math.gcd(span_width // groups, max(1, 128 // groups))
    block_width = repeats * groups
    diagonal = jnp.einsum(
        "ab,yxij->yxaibj", jnp.eye(repeats, dtype=jnp.float32), source_kernel.astype(jnp.float32)
    )
    diagonal = diagonal.reshape(3, 3, block_width, block_width).astype(jnp.bfloat16)
    running = jnp.zeros((neighbours[1].size // block_width, block_width), jnp.float32)
    for offset in range(3):
        window = bordered[:, offset : offset + window_rows].reshape(3, -1, block_width)
        running = running + jnp.einsum(
            "xmc,xcd->md", window, diagonal[offset], preferred_element_type=jnp.float32
        )
    return jnp.maximum(running, 0.0).astype(jnp.bfloat16).reshape(neighbours[1].shape)


def local(
    source_features,
    target_features,
    source_rows,
    target_cols,
    target_kernel_one,
    source_kernel,
    target_kernel_two,
):
    groups = source_kernel.shape[2]
    channels = source_features.shape[2] // groups
    window_rows = source_rows.shape[0]
    selected = jnp.take(source_features[:, 0], source_rows, axis=0)
    columns = selected[None]
    column_count = columns.shape[0]
    columns = columns.reshape(column_count, window_rows, groups, channels)
    gathered = lax.all_gather(target_features, "src", axis=1, tiled=True)
    gathered = jnp.take(gathered, target_cols, axis=1)
    target_rows = gathered.shape[0]
    breadth = gathered.shape[1]
    grouped = gathered.reshape(target_rows, breadth, groups, channels)
    volume = jnp.einsum("khgc,rwgc->khrwg", columns, grouped, preferred_element_type=jnp.float32)
    volume = (
        (volume * channels ** (-0.5))
        .astype(jnp.bfloat16)
        .reshape(column_count * window_rows, target_rows, breadth * groups)
    )
    padded = with_halo(volume, (("tgt", 1),), 1)
    filtered_one = target_pass(padded, build_toeplitz(target_kernel_one, breadth))
    neighbours = with_halo(filtered_one[None], (("src", 0),), 1)
    filtered_two = column_filter(neighbours, source_kernel, groups, window_rows)
    padded_last = with_halo(filtered_two, (("tgt", 1),), 1)
    filtered_three = target_pass(padded_last, build_toeplitz(target_kernel_two, breadth))
    return filtered_three[:, None]


def solution(mesh):
    def step(*args):
        source, target, source_rows, cols, _, source_kernel, _ = args
        count = lax.axis_size("src")
        fits = (
            lax.axis_size("tgt") == 2
            and count > 1
            and count & (count - 1) == 0
            and source.shape[1] == 1
            and target.shape[1] == 1
            and cols.shape[0] == count
            and count * source_kernel.shape[2] == LANES
            and source_rows.shape[0] <= TILE
            and target.shape[0] % (2 * TILE) == 0
        )
        return (fast_local if fits else local)(*args)

    return jax.shard_map(
        step,
        mesh=mesh,
        in_specs=(
            P("pair", "src", None),
            P(("pair", "tgt"), "src", None),
            P("pair"),
            P("pair"),
            P(),
            P(),
            P(),
        ),
        out_specs=P("pair", "src", "tgt", None),
        check_vma=False,
    )
```

```python
import functools
import math

import jax
import jax.numpy as jnp
from jax import lax
from jax.experimental import pallas as pl
from jax.experimental.pallas import tpu as pltpu
from jax.sharding import PartitionSpec as P


LANES = 128
TILE = 8


def rounds_of(count):
    rounds = []
    while count > 4:
        count //= 2
        rounds.append([(count, count)])
    rounds.append([(1, 2), (2, 1), (3, 3)] if count == 4 else [(1, 1)])
    return rounds


def entries_of(count):
    *early, last = rounds_of(count)
    held = [(0, 0)]
    for ((mask, _),) in early:
        held = held + [(offset ^ mask, hops + 1) for offset, hops in held]
    entries = [(0, 0, k, (offset, offset), hops) for k, (offset, hops) in enumerate(held)]
    for part, (sent_0, sent_1) in enumerate(last):
        twin = last.index((sent_1, sent_0))
        entries += [
            (part + 1, twin + 1, k, (offset ^ sent_1, offset ^ sent_0), hops + 1)
            for k, (offset, hops) in enumerate(held)
        ]
    return entries


def pack_kernel(count, rows_hbm, source_hbm, target_hbm, *refs):
    kernels, (out_ref, *held), (rows_ref, source_ref, wide_ref, sems) = (
        refs[:count],
        refs[count : 2 * count + 1],
        refs[2 * count + 1 :],
    )
    rows = target_hbm.shape[0]
    window = rows_hbm.shape[0]
    copies = [
        pltpu.make_async_copy(source, target, sems.at[index])
        for index, (source, target) in enumerate(
            [
                (rows_hbm, rows_ref),
                (source_hbm, source_ref),
                (target_hbm, out_ref.at[0, pl.ds(0, rows)]),
                *zip(kernels, held, strict=True),
            ]
        )
    ]
    for copy in copies:
        copy.start()
    copies[1].wait()
    wide_ref[...] = source_ref[...].astype(jnp.float32)
    copies[0].wait()
    lines = [wide_ref[pl.ds(rows_ref[h], 1), :] for h in range(window)]
    blank = out_ref.shape[1] - rows - window
    if blank:
        lines.append(jnp.zeros((blank, wide_ref.shape[1]), jnp.float32))
    out_ref[0, rows:, :] = jnp.concatenate(lines, axis=0).astype(out_ref.dtype)
    for copy in copies[2:]:
        copy.wait()


def pack(source_rows, source, target, kernels, height):
    operands = (source_rows, source, target, *kernels)
    out, *held = pl.pallas_call(
        functools.partial(pack_kernel, len(kernels)),
        out_shape=[
            jax.ShapeDtypeStruct((1, height, target.shape[1]), target.dtype),
            *(jax.ShapeDtypeStruct(kernel.shape, kernel.dtype) for kernel in kernels),
        ],
        in_specs=[pl.BlockSpec(memory_space=pltpu.HBM)] * len(operands),
        out_specs=[pl.BlockSpec(memory_space=pltpu.VMEM)] * (1 + len(kernels)),
        scratch_shapes=[
            pltpu.SMEM(source_rows.shape, source_rows.dtype),
            pltpu.VMEM(source.shape, source.dtype),
            pltpu.VMEM(source.shape, jnp.float32),
            pltpu.SemaphoreType.DMA((3 + len(kernels),)),
        ],
        compiler_params=pltpu.CompilerParams(vmem_limit_bytes=4 << 20),
        name="pack",
    )(*(pltpu.with_memory_space_constraint(x, pltpu.HBM) for x in operands))
    return out, held


def widen(block):
    return jnp.concatenate(
        [
            block.astype(jnp.float32),
            jnp.zeros((block.shape[0], LANES - block.shape[1]), jnp.float32),
        ],
        axis=1,
    )


def band_rows(kernel_ref, a, place, breadth):
    groups = kernel_ref.shape[2]
    total = jnp.zeros((groups, LANES), jnp.float32)
    for b in range(3):
        out_place = place - b + 1
        if 0 <= out_place < breadth:
            piece = widen(kernel_ref[a, b])
            total = total + (pltpu.roll(piece, out_place * groups, 1) if out_place else piece)
    return total


def weights_kernel(offsets, cols_ref, one_ref, source_ref, two_ref, band_one, blocks, band_two):
    groups = one_ref.shape[2]
    breadth = LANES // groups
    here = lax.axis_index("src")
    first = lax.axis_index("tgt") == 0
    for place in range(breadth):
        offset = jnp.bitwise_xor(cols_ref[place], here)
        entry = 0
        for index, (on_0, on_1) in enumerate(offsets):
            entry = jnp.where(offset == jnp.where(first, on_0, on_1), index, entry)
        start = pl.multiple_of(entry * groups, groups)
        for a in range(3):
            lanes = slice(a * LANES, (a + 1) * LANES)
            band_one[pl.ds(start, groups), lanes] = band_rows(one_ref, a, place, breadth).astype(
                band_one.dtype
            )
            row = a * LANES + place * groups
            band_two[row : row + groups, :] = band_rows(two_ref, a, place, breadth).astype(
                band_two.dtype
            )
            for b in range(3):
                piece = widen(source_ref[a, b])
                piece = pltpu.roll(piece, place * groups, 1) if place else piece
                row = b * LANES + place * groups
                blocks[row : row + groups, lanes] = piece.astype(blocks.dtype)


def weights(target_cols, one, source, two, offsets):
    smem = pl.BlockSpec(memory_space=pltpu.SMEM)
    vmem = pl.BlockSpec(memory_space=pltpu.VMEM)
    return pl.pallas_call(
        functools.partial(weights_kernel, offsets),
        out_shape=[
            jax.ShapeDtypeStruct((LANES, 3 * LANES), one.dtype),
            jax.ShapeDtypeStruct((3 * LANES, 3 * LANES), one.dtype),
            jax.ShapeDtypeStruct((3 * LANES, LANES), one.dtype),
        ],
        in_specs=[smem, vmem, vmem, vmem],
        out_specs=[vmem, vmem, vmem],
        compiler_params=pltpu.CompilerParams(vmem_limit_bytes=4 << 20),
        name="weights",
    )(target_cols, one, source, two)


def shifted_sum(product):
    rows = product.shape[0]
    below = pltpu.roll(product[:, :LANES], 1, 0)
    above = pltpu.roll(product[:, 2 * LANES :], rows - 1, 0)
    return below + product[:, LANES : 2 * LANES] + above


def row_taps(plane):
    rows = plane.shape[0]
    return jnp.concatenate([pltpu.roll(plane, 1, 0), plane, pltpu.roll(plane, rows - 1, 0)], axis=1)


def swap_lane_groups(arrays, groups):
    lane_group = lax.broadcasted_iota(jnp.int32, arrays[0].shape, 1) // groups
    bit = len(arrays) // 2
    while bit:
        lower = (lane_group // bit) % 2 == 0
        result = list(arrays)
        for index in range(len(arrays)):
            if index & bit:
                continue
            low, high = arrays[index], arrays[index | bit]
            result[index] = jnp.where(lower, low, pltpu.roll(high, bit * groups, 1))
            result[index | bit] = jnp.where(lower, pltpu.roll(low, LANES - bit * groups, 1), high)
        arrays = result
        bit //= 2
    return arrays


def planes_of(product, count, planes, groups):
    rows = product.shape[0] // count
    result = []
    for start in range(0, planes, count):
        lanes = min(1 << (planes - start - 1).bit_length(), count)
        blocks = [
            product[entry * rows : (entry + 1) * rows, start * groups : (start + lanes) * groups]
            for entry in range(count)
        ]
        stack = [
            jnp.concatenate(blocks[low::lanes], axis=1) if lanes < count else blocks[low]
            for low in range(lanes)
        ]
        result += swap_lane_groups(stack, groups)[: planes - start]
    return result


def planes_padded(planes, count):
    left = planes % count
    return planes - left + (1 << (left - 1).bit_length() if left else 0)


class Block:
    def __init__(self, rows):
        self.rows = rows
        self.first = lax.axis_index("tgt") == 0
        self.outside_from = jnp.where(self.first, TILE - 2, 0)

    def beside(self, other):
        return jnp.where(
            self.first,
            other[: TILE, :].astype(jnp.float32),
            other[self.rows - TILE : self.rows, :].astype(jnp.float32),
        )

    def keep_inside(self, tiles):
        row = lax.broadcasted_iota(jnp.int32, tiles.shape, 0) % TILE
        outside = (row >= self.outside_from) & (row < self.outside_from + 2)
        return jnp.where(outside, 0.0, tiles)


def correlate(columns, spread, channels):
    product = lax.dot_general(
        columns, spread, (((1,), (1,)), ((), ())), preferred_element_type=jnp.float32
    )
    return product * channels ** (-0.5)


def volume_kernel(entries, groups, window, *refs):
    *parts, base_ref, edge_ref, spread_ref = refs
    count = len(entries)
    width = parts[0].shape[2]
    planes = 3 * window
    rows = base_ref.shape[0] // planes
    channels = width // groups
    here = lax.axis_index("src")
    block = Block(rows)
    first = block.first
    half = (len(parts) + 1) // 2
    near = [parts[part].at[k] for part, _, k, _, _ in entries]
    far = [
        parts[half + twin].at[k] if half + twin < len(parts) else parts[part].at[k]
        for part, twin, k, _, _ in entries
    ]

    def source_rows(entry):
        return near[entry][rows : rows + TILE, :].astype(jnp.float32)

    before = jnp.zeros((TILE, width), jnp.float32)
    after = jnp.zeros((TILE, width), jnp.float32)
    for entry, (_, _, _, (on_0, on_1), _) in enumerate(entries):
        if any(o & (o + 1) == 0 and o for o in (on_0, on_1)):
            offset = jnp.where(first, on_0, on_1)
            candidate = source_rows(entry)
            before = jnp.where(jnp.bitwise_xor(here, here - 1) == offset, candidate, before)
            after = jnp.where(jnp.bitwise_xor(here, here + 1) == offset, candidate, after)
    row_group = lax.broadcasted_iota(jnp.int32, (groups, width), 0)
    own_group = row_group == lax.broadcasted_iota(jnp.int32, (groups, width), 1) // channels
    spread = []
    for part in (before, source_rows(0), after):
        for h in range(window):
            line = jnp.broadcast_to(part[h : h + 1, :], (groups, width))
            spread.append(jnp.where(own_group, line, 0.0))
    spread += [jnp.zeros((groups, width), jnp.float32)] * (planes_padded(planes, count) - planes)
    spread = jnp.concatenate(spread, axis=0).astype(jnp.bfloat16)
    spread_ref[...] = spread

    base, edge = [], []
    for entry in range(count):
        mine, other = near[entry], far[entry]
        if entries[entry][4] % 2:
            mine, other = other, mine
        base.append(mine[:rows, :])
        edge.append(block.beside(other))
    base = correlate(jnp.concatenate(base, axis=0), spread, channels).astype(base_ref.dtype)
    edge = jnp.concatenate(edge, axis=0).astype(jnp.bfloat16)
    edge = block.keep_inside(correlate(edge, spread, channels))
    base_ref[...] = jnp.concatenate(planes_of(base, count, planes, groups), axis=0)
    edge_ref[...] = jnp.concatenate(planes_of(edge, count, planes, groups), axis=0)


def with_column(stacked, product, column, planes, groups):
    rows = product.shape[0]
    short = -product.shape[1] % LANES
    if short:
        product = jnp.concatenate([product, jnp.zeros((rows, short), product.dtype)], axis=1)
    here = lax.broadcasted_iota(jnp.int32, (rows, LANES), 1) // groups == column
    result = []
    for plane in range(planes):
        tile, place = divmod(plane * groups, LANES)
        piece = product[:, tile * LANES : (tile + 1) * LANES]
        shift = (column * groups - place) % LANES
        piece = pltpu.roll(piece, shift, 1) if shift else piece
        result.append(jnp.where(here, piece, stacked[plane]))
    return result


def filter_kernel(entries, groups, window, base_ref, edge_ref, spread_ref, last_ref, *refs):
    band_one, blocks, band_two, out_ref = refs
    rows = out_ref.shape[1]
    high = rows + TILE
    planes = 3 * window
    channels = spread_ref.shape[1] // groups
    block = Block(rows)
    spread = spread_ref[...]
    last = max(part for part, _, _, _, _ in entries)
    base = [base_ref[plane * rows : (plane + 1) * rows, :] for plane in range(planes)]
    edge = [edge_ref[plane * TILE : (plane + 1) * TILE, :] for plane in range(planes)]
    for column, (part, _, k, _, hops) in enumerate(entries):
        if part != last:
            continue
        brought = last_ref.at[k]
        if hops % 2:
            product = correlate(brought[:rows, :], spread, channels).astype(base_ref.dtype)
            base = with_column(base, product, column, planes, groups)
        else:
            product = correlate(block.beside(brought).astype(jnp.bfloat16), spread, channels)
            edge = with_column(edge, block.keep_inside(product), column, planes, groups)
    base = jnp.concatenate(base, axis=0)
    edge = jnp.concatenate(edge, axis=0).astype(jnp.bfloat16)

    base = jnp.dot(base, band_one[...], preferred_element_type=jnp.float32)
    edge = jnp.dot(edge, band_one[...], preferred_element_type=jnp.float32)
    one = []
    for plane in range(planes):
        product = jnp.concatenate(
            [base[plane * rows : (plane + 1) * rows], edge[plane * TILE : (plane + 1) * TILE]],
            axis=0,
        )
        total = jnp.maximum(shifted_sum(product), 0.0)
        one += [total[:rows], block.keep_inside(total[rows:])]
    one = jnp.concatenate(one, axis=0).astype(jnp.bfloat16).reshape(3, window * high, LANES)
    product = jnp.dot(
        jnp.concatenate([one[0], one[1], one[2]], axis=1),
        blocks[...],
        preferred_element_type=jnp.float32,
    )
    product = product.reshape(window, high, 3 * LANES)
    two = []
    for h in range(window):
        total = product[h, :, LANES : 2 * LANES]
        if h > 0:
            total = total + product[h - 1, :, :LANES]
        if h < window - 1:
            total = total + product[h + 1, :, 2 * LANES :]
        two.append(jnp.maximum(total, 0.0))
    taps = jnp.concatenate([row_taps(plane) for plane in two], axis=0).astype(jnp.bfloat16)
    three = jnp.dot(taps, band_two[...], preferred_element_type=jnp.float32)
    three = three.reshape(window, high, LANES)[:, :rows]
    out_ref[...] = jnp.maximum(three, 0.0).astype(out_ref.dtype)


def local_call(kernel, out_shape, *operands):
    vmem = pl.BlockSpec(memory_space=pltpu.VMEM)
    return pl.pallas_call(
        kernel,
        out_shape=out_shape,
        in_specs=[vmem] * len(operands),
        out_specs=jax.tree.map(lambda _: vmem, out_shape),
        compiler_params=pltpu.CompilerParams(vmem_limit_bytes=8 << 20),
    )(*operands)


def filter_all(near, far, matrices, entries, groups, window, rows):
    *far, last = far
    planes = 3 * window
    width = near[0].shape[2]
    volume = local_call(
        functools.partial(volume_kernel, entries, groups, window),
        [
            jax.ShapeDtypeStruct((planes * rows, LANES), jnp.bfloat16),
            jax.ShapeDtypeStruct((planes * TILE, LANES), jnp.float32),
            jax.ShapeDtypeStruct(
                (planes_padded(planes, LANES // groups) * groups, width), jnp.bfloat16
            ),
        ],
        *near,
        *far,
    )
    return local_call(
        functools.partial(filter_kernel, entries, groups, window),
        jax.ShapeDtypeStruct((window, rows, LANES), jnp.bfloat16),
        *volume,
        last,
        *matrices,
    )


def fast_local(
    source_features,
    target_features,
    source_rows,
    target_cols,
    target_kernel_one,
    source_kernel,
    target_kernel_two,
):
    groups = source_kernel.shape[2]
    window = source_rows.shape[0]
    rows = target_features.shape[0]
    count = lax.axis_size("src")
    entries = entries_of(count)
    height = rows + -(-window // TILE) * TILE

    def exchange(block, mask):
        pairs = [(2 * s + t, 2 * (s ^ mask[t]) + 1 - t) for s in range(count) for t in range(2)]
        return lax.ppermute(block, ("src", "tgt"), pairs)

    held, kernels = pack(
        source_rows,
        source_features[:, 0],
        target_features[:, 0],
        (target_cols, target_kernel_one, source_kernel, target_kernel_two),
        height,
    )
    *early, last = rounds_of(count)
    matrices = None
    for ((mask, _),) in early:
        arrived = exchange(held, (mask, mask))
        if matrices is None:
            matrices = weights(*kernels, [offsets for _, _, _, offsets, _ in entries])
            arrived, matrices = lax.optimization_barrier((arrived, matrices))
        held = jnp.concatenate([held, arrived], axis=0)
    if matrices is None:
        matrices = weights(*kernels, [offsets for _, _, _, offsets, _ in entries])
    near = [held, *(exchange(held, mask) for mask in last)]
    far = [exchange(part, (0, 0)) for part in near]
    return filter_all(near, far, matrices, entries, groups, window, rows)[:, None]


def with_halo(block, sides, width):
    for axis, dim in sides:
        count = lax.axis_size(axis)
        forward = [(i, i + 1) for i in range(count - 1)]
        backward = [(target, source) for source, target in forward]
        low = lax.ppermute(
            lax.slice_in_dim(block, block.shape[dim] - width, None, axis=dim), axis, forward
        )
        high = lax.ppermute(lax.slice_in_dim(block, 0, width, axis=dim), axis, backward)
        block = jnp.concatenate([low, block, high], axis=dim)
    return block


def build_toeplitz(kernel, breadth):
    groups = kernel.shape[2]
    span_width = breadth * groups
    row_index = lax.broadcasted_iota(jnp.int32, (3, breadth, breadth), 1)
    col_index = lax.broadcasted_iota(jnp.int32, (3, breadth, breadth), 2)
    tap_index = lax.broadcasted_iota(jnp.int32, (3, breadth, breadth), 0)
    shifts = (row_index - col_index == tap_index - 1).astype(jnp.bfloat16)
    matrices = []
    for offset_y in range(3):
        banded = jnp.einsum(
            "xab,xio->aibo", shifts, kernel[offset_y], preferred_element_type=jnp.float32
        )
        matrices.append(banded.astype(jnp.bfloat16).reshape(span_width, span_width))
    return jnp.stack(matrices)


def banded_pass(slices, matrices):
    span_width = matrices.shape[1]
    running = jnp.dot(
        slices[0].reshape(-1, span_width), matrices[0], preferred_element_type=jnp.float32
    )
    for offset in range(1, 3):
        running = running + jnp.dot(
            slices[offset].reshape(-1, span_width),
            matrices[offset],
            preferred_element_type=jnp.float32,
        )
    return jnp.maximum(running, 0.0).astype(jnp.bfloat16).reshape(slices[0].shape)


def target_pass(padded, matrices):
    row_count = padded.shape[1] - 2
    return banded_pass([padded[:, offset : offset + row_count] for offset in range(3)], matrices)


def column_filter(neighbours, source_kernel, groups, window_rows):
    bordered = jnp.pad(neighbours, ((0, 0), (1, 1), (0, 0), (0, 0)))
    span_width = neighbours.shape[3]
    repeats = math.gcd(span_width // groups, max(1, 128 // groups))
    block_width = repeats * groups
    diagonal = jnp.einsum(
        "ab,yxij->yxaibj", jnp.eye(repeats, dtype=jnp.float32), source_kernel.astype(jnp.float32)
    )
    diagonal = diagonal.reshape(3, 3, block_width, block_width).astype(jnp.bfloat16)
    running = jnp.zeros((neighbours[1].size // block_width, block_width), jnp.float32)
    for offset in range(3):
        window = bordered[:, offset : offset + window_rows].reshape(3, -1, block_width)
        running = running + jnp.einsum(
            "xmc,xcd->md", window, diagonal[offset], preferred_element_type=jnp.float32
        )
    return jnp.maximum(running, 0.0).astype(jnp.bfloat16).reshape(neighbours[1].shape)


def local(
    source_features,
    target_features,
    source_rows,
    target_cols,
    target_kernel_one,
    source_kernel,
    target_kernel_two,
):
    groups = source_kernel.shape[2]
    channels = source_features.shape[2] // groups
    window_rows = source_rows.shape[0]
    selected = jnp.take(source_features[:, 0], source_rows, axis=0)
    columns = selected[None]
    column_count = columns.shape[0]
    columns = columns.reshape(column_count, window_rows, groups, channels)
    gathered = lax.all_gather(target_features, "src", axis=1, tiled=True)
    gathered = jnp.take(gathered, target_cols, axis=1)
    target_rows = gathered.shape[0]
    breadth = gathered.shape[1]
    grouped = gathered.reshape(target_rows, breadth, groups, channels)
    volume = jnp.einsum("khgc,rwgc->khrwg", columns, grouped, preferred_element_type=jnp.float32)
    volume = (
        (volume * channels ** (-0.5))
        .astype(jnp.bfloat16)
        .reshape(column_count * window_rows, target_rows, breadth * groups)
    )
    padded = with_halo(volume, (("tgt", 1),), 1)
    filtered_one = target_pass(padded, build_toeplitz(target_kernel_one, breadth))
    neighbours = with_halo(filtered_one[None], (("src", 0),), 1)
    filtered_two = column_filter(neighbours, source_kernel, groups, window_rows)
    padded_last = with_halo(filtered_two, (("tgt", 1),), 1)
    filtered_three = target_pass(padded_last, build_toeplitz(target_kernel_two, breadth))
    return filtered_three[:, None]


def solution(mesh):
    def step(*args):
        source, target, source_rows, cols, _, source_kernel, _ = args
        count = lax.axis_size("src")
        fits = (
            lax.axis_size("tgt") == 2
            and count > 1
            and count & (count - 1) == 0
            and source.shape[1] == 1
            and target.shape[1] == 1
            and cols.shape[0] == count
            and count * source_kernel.shape[2] == LANES
            and source_rows.shape[0] <= TILE
            and target.shape[0] % (2 * TILE) == 0
        )
        return (fast_local if fits else local)(*args)

    return jax.shard_map(
        step,
        mesh=mesh,
        in_specs=(
            P("pair", "src", None),
            P(("pair", "tgt"), "src", None),
            P("pair"),
            P("pair"),
            P(),
            P(),
            P(),
        ),
        out_specs=P("pair", "src", "tgt", None),
        check_vma=False,
    )
```

```python
import functools
import math

import jax
import jax.numpy as jnp
from jax import lax
from jax.experimental import pallas as pl
from jax.experimental.pallas import tpu as pltpu
from jax.sharding import PartitionSpec as P


LANES = 128
TILE = 8


def whole_tiles(rows):
    return -(-rows // TILE) * TILE


def rounds_of(count):
    rounds = []
    while count > 4:
        count //= 2
        rounds.append([(count, count)])
    rounds.append([(1, 2), (2, 1), (3, 3)] if count == 4 else [(1, 1)])
    return rounds


def entries_of(count):
    *early, last = rounds_of(count)
    held = [(0, 0)]
    for ((mask, _),) in early:
        held = held + [(offset ^ mask, hops + 1) for offset, hops in held]
    entries = [(0, 0, k, (offset, offset), hops) for k, (offset, hops) in enumerate(held)]
    for part, (sent_0, sent_1) in enumerate(last):
        twin = last.index((sent_1, sent_0))
        entries += [
            (part + 1, twin + 1, k, (offset ^ sent_1, offset ^ sent_0), hops + 1)
            for k, (offset, hops) in enumerate(held)
        ]
    return entries


def fetch(pairs, sems):
    copies = [
        pltpu.make_async_copy(source, target, sems.at[index])
        for index, (source, target) in enumerate(pairs)
    ]
    for copy in copies:
        copy.start()
    return copies


def pack_kernel(rows_hbm, source_hbm, target_hbm, out_ref, rows_ref, source_ref, wide_ref, sems):
    rows = target_hbm.shape[0]
    window = rows_hbm.shape[0]
    copies = fetch(
        [
            (rows_hbm, rows_ref),
            (source_hbm, source_ref),
            (target_hbm, out_ref.at[pl.ds(0, rows)]),
        ],
        sems,
    )
    copies[1].wait()
    wide_ref[...] = source_ref[...].astype(jnp.float32)
    copies[0].wait()
    lines = [wide_ref[pl.ds(rows_ref[h], 1), :] for h in range(window)]
    blank = out_ref.shape[0] - rows - window
    if blank:
        lines.append(jnp.zeros((blank, wide_ref.shape[1]), jnp.float32))
    out_ref[rows:, :] = jnp.concatenate(lines, axis=0).astype(out_ref.dtype)
    copies[2].wait()


def from_hbm(kernel, out_shape, operands, scratch):
    return pl.pallas_call(
        kernel,
        out_shape=out_shape,
        in_specs=[pl.BlockSpec(memory_space=pltpu.HBM)] * len(operands),
        out_specs=jax.tree.map(lambda _: pl.BlockSpec(memory_space=pltpu.VMEM), out_shape),
        scratch_shapes=[*scratch, pltpu.SemaphoreType.DMA((len(operands),))],
        compiler_params=pltpu.CompilerParams(vmem_limit_bytes=4 << 20),
    )(*(pltpu.with_memory_space_constraint(x, pltpu.HBM) for x in operands))


def pack(source_rows, source, target):
    height = target.shape[0] + whole_tiles(source_rows.shape[0])
    return from_hbm(
        pack_kernel,
        jax.ShapeDtypeStruct((height, target.shape[1]), target.dtype),
        (source_rows, source, target),
        [
            pltpu.SMEM(source_rows.shape, source_rows.dtype),
            pltpu.VMEM(source.shape, source.dtype),
            pltpu.VMEM(source.shape, jnp.float32),
        ],
    )


def widen(block):
    return jnp.concatenate(
        [
            block.astype(jnp.float32),
            jnp.zeros((block.shape[0], LANES - block.shape[1]), jnp.float32),
        ],
        axis=1,
    )


def band_rows(kernel_ref, a, place, breadth):
    groups = kernel_ref.shape[2]
    total = jnp.zeros((groups, LANES), jnp.float32)
    for b in range(3):
        out_place = place - b + 1
        if 0 <= out_place < breadth:
            piece = widen(kernel_ref[a, b])
            total = total + (pltpu.roll(piece, out_place * groups, 1) if out_place else piece)
    return total


def weights_kernel(offsets, *refs):
    operands, (band_one, blocks, band_two), (*scratch, sems) = refs[:4], refs[4:7], refs[7:]
    cols_ref, one_ref, source_ref, two_ref = scratch
    for copy in fetch(zip(operands, scratch, strict=True), sems):
        copy.wait()
    groups = one_ref.shape[2]
    breadth = LANES // groups
    here = lax.axis_index("src")
    first = lax.axis_index("tgt") == 0
    for place in range(breadth):
        offset = jnp.bitwise_xor(cols_ref[place], here)
        entry = 0
        for index, (on_0, on_1) in enumerate(offsets):
            entry = jnp.where(offset == jnp.where(first, on_0, on_1), index, entry)
        start = pl.multiple_of(entry * groups, groups)
        for a in range(3):
            lanes = slice(a * LANES, (a + 1) * LANES)
            band_one[pl.ds(start, groups), lanes] = band_rows(one_ref, a, place, breadth).astype(
                band_one.dtype
            )
            row = a * LANES + place * groups
            band_two[row : row + groups, :] = band_rows(two_ref, a, place, breadth).astype(
                band_two.dtype
            )
            for b in range(3):
                piece = widen(source_ref[a, b])
                piece = pltpu.roll(piece, place * groups, 1) if place else piece
                row = b * LANES + place * groups
                blocks[row : row + groups, lanes] = piece.astype(blocks.dtype)


def weights(target_cols, kernels, offsets):
    dtype = kernels[0].dtype
    return from_hbm(
        functools.partial(weights_kernel, offsets),
        [
            jax.ShapeDtypeStruct((LANES, 3 * LANES), dtype),
            jax.ShapeDtypeStruct((3 * LANES, 3 * LANES), dtype),
            jax.ShapeDtypeStruct((3 * LANES, LANES), dtype),
        ],
        (target_cols, *kernels),
        [
            pltpu.SMEM(target_cols.shape, target_cols.dtype),
            *(pltpu.VMEM(kernel.shape, kernel.dtype) for kernel in kernels),
        ],
    )


def shifted_sum(product):
    rows = product.shape[0]
    below = pltpu.roll(product[:, :LANES], 1, 0)
    above = pltpu.roll(product[:, 2 * LANES :], rows - 1, 0)
    return below + product[:, LANES : 2 * LANES] + above


def row_taps(plane):
    rows = plane.shape[0]
    return jnp.concatenate([pltpu.roll(plane, 1, 0), plane, pltpu.roll(plane, rows - 1, 0)], axis=1)


def swap_lane_groups(arrays, groups):
    lane_group = lax.broadcasted_iota(jnp.int32, arrays[0].shape, 1) // groups
    bit = len(arrays) // 2
    while bit:
        lower = (lane_group // bit) % 2 == 0
        result = list(arrays)
        for index in range(len(arrays)):
            if index & bit:
                continue
            low, high = arrays[index], arrays[index | bit]
            result[index] = jnp.where(lower, low, pltpu.roll(high, bit * groups, 1))
            result[index | bit] = jnp.where(lower, pltpu.roll(low, LANES - bit * groups, 1), high)
        arrays = result
        bit //= 2
    return arrays


def planes_of(product, count, planes, groups):
    rows = product.shape[0] // count
    result = []
    for start in range(0, planes, count):
        lanes = min(1 << (planes - start - 1).bit_length(), count)
        blocks = [
            product[entry * rows : (entry + 1) * rows, start * groups : (start + lanes) * groups]
            for entry in range(count)
        ]
        stack = [
            jnp.concatenate(blocks[low::lanes], axis=1) if lanes < count else blocks[low]
            for low in range(lanes)
        ]
        result += swap_lane_groups(stack, groups)[: planes - start]
    return result


def planes_padded(planes, count):
    left = planes % count
    return planes - left + (1 << (left - 1).bit_length() if left else 0)


class Block:
    def __init__(self, rows):
        self.rows = rows
        self.first = lax.axis_index("tgt") == 0
        self.outside_from = jnp.where(self.first, TILE - 2, 0)

    def beside(self, other):
        return jnp.where(
            self.first,
            other[: TILE, :].astype(jnp.float32),
            other[self.rows - TILE : self.rows, :].astype(jnp.float32),
        )

    def keep_inside(self, tiles):
        row = lax.broadcasted_iota(jnp.int32, tiles.shape, 0) % TILE
        outside = (row >= self.outside_from) & (row < self.outside_from + 2)
        return jnp.where(outside, 0.0, tiles)


def correlate(columns, spread, channels):
    product = lax.dot_general(
        columns, spread, (((1,), (1,)), ((), ())), preferred_element_type=jnp.float32
    )
    return product * channels ** (-0.5)


def volume_kernel(entries, groups, window, *refs):
    *parts, base_ref, edge_ref, spread_ref = refs
    count = len(entries)
    width = parts[0].shape[1]
    planes = 3 * window
    rows = base_ref.shape[0] // planes
    channels = width // groups
    here = lax.axis_index("src")
    block = Block(rows)
    first = block.first
    half = (len(parts) + 1) // 2
    held = 1 + max(k for _, _, k, _, _ in entries)
    near = [parts[part].at[pl.ds(k * rows, rows)] for part, _, k, _, _ in entries]
    far = [
        parts[half + twin if half + twin < len(parts) else part].at[pl.ds(k * rows, rows)]
        for part, twin, k, _, _ in entries
    ]

    def source_rows(entry):
        part, _, k, _, _ = entries[entry]
        lines = parts[part][held * rows :, :].astype(jnp.float32)
        return lines[k * window : (k + 1) * window]

    before = jnp.zeros((window, width), jnp.float32)
    after = jnp.zeros((window, width), jnp.float32)
    for entry, (_, _, _, (on_0, on_1), _) in enumerate(entries):
        if any(o & (o + 1) == 0 and o for o in (on_0, on_1)):
            offset = jnp.where(first, on_0, on_1)
            candidate = source_rows(entry)
            before = jnp.where(jnp.bitwise_xor(here, here - 1) == offset, candidate, before)
            after = jnp.where(jnp.bitwise_xor(here, here + 1) == offset, candidate, after)
    row_group = lax.broadcasted_iota(jnp.int32, (groups, width), 0)
    own_group = row_group == lax.broadcasted_iota(jnp.int32, (groups, width), 1) // channels
    spread = []
    for part in (before, source_rows(0), after):
        for h in range(window):
            line = jnp.broadcast_to(part[h : h + 1, :], (groups, width))
            spread.append(jnp.where(own_group, line, 0.0))
    spread += [jnp.zeros((groups, width), jnp.float32)] * (planes_padded(planes, count) - planes)
    spread = jnp.concatenate(spread, axis=0).astype(jnp.bfloat16)
    spread_ref[...] = spread

    base, edge = [], []
    for entry in range(count):
        mine, other = near[entry], far[entry]
        if entries[entry][4] % 2:
            mine, other = other, mine
        base.append(mine[:rows, :])
        edge.append(block.beside(other))
    base = correlate(jnp.concatenate(base, axis=0), spread, channels).astype(base_ref.dtype)
    edge = jnp.concatenate(edge, axis=0).astype(jnp.bfloat16)
    edge = block.keep_inside(correlate(edge, spread, channels))
    base_ref[...] = jnp.concatenate(planes_of(base, count, planes, groups), axis=0)
    edge_ref[...] = jnp.concatenate(planes_of(edge, count, planes, groups), axis=0)


def with_column(stacked, product, column, planes, groups):
    rows = product.shape[0]
    short = -product.shape[1] % LANES
    if short:
        product = jnp.concatenate([product, jnp.zeros((rows, short), product.dtype)], axis=1)
    here = lax.broadcasted_iota(jnp.int32, (rows, LANES), 1) // groups == column
    result = []
    for plane in range(planes):
        tile, place = divmod(plane * groups, LANES)
        piece = product[:, tile * LANES : (tile + 1) * LANES]
        shift = (column * groups - place) % LANES
        piece = pltpu.roll(piece, shift, 1) if shift else piece
        result.append(jnp.where(here, piece, stacked[plane]))
    return result


def filter_kernel(entries, groups, window, base_ref, edge_ref, spread_ref, last_ref, *refs):
    band_one, blocks, band_two, out_ref = refs
    rows = out_ref.shape[1]
    high = rows + TILE
    planes = 3 * window
    channels = spread_ref.shape[1] // groups
    block = Block(rows)
    spread = spread_ref[...]
    last = max(part for part, _, _, _, _ in entries)
    base = [base_ref[plane * rows : (plane + 1) * rows, :] for plane in range(planes)]
    edge = [edge_ref[plane * TILE : (plane + 1) * TILE, :] for plane in range(planes)]
    for column, (part, _, k, _, hops) in enumerate(entries):
        if part != last:
            continue
        brought = last_ref.at[pl.ds(k * rows, rows)]
        if hops % 2:
            product = correlate(brought[:rows, :], spread, channels).astype(base_ref.dtype)
            base = with_column(base, product, column, planes, groups)
        else:
            product = correlate(block.beside(brought).astype(jnp.bfloat16), spread, channels)
            edge = with_column(edge, block.keep_inside(product), column, planes, groups)
    base = jnp.concatenate(base, axis=0)
    edge = jnp.concatenate(edge, axis=0).astype(jnp.bfloat16)

    base = jnp.dot(base, band_one[...], preferred_element_type=jnp.float32)
    edge = jnp.dot(edge, band_one[...], preferred_element_type=jnp.float32)
    one = []
    for plane in range(planes):
        product = jnp.concatenate(
            [base[plane * rows : (plane + 1) * rows], edge[plane * TILE : (plane + 1) * TILE]],
            axis=0,
        )
        total = jnp.maximum(shifted_sum(product), 0.0)
        one += [total[:rows], block.keep_inside(total[rows:])]
    one = jnp.concatenate(one, axis=0).astype(jnp.bfloat16).reshape(3, window * high, LANES)
    product = jnp.dot(
        jnp.concatenate([one[0], one[1], one[2]], axis=1),
        blocks[...],
        preferred_element_type=jnp.float32,
    )
    product = product.reshape(window, high, 3 * LANES)
    two = []
    for h in range(window):
        total = product[h, :, LANES : 2 * LANES]
        if h > 0:
            total = total + product[h - 1, :, :LANES]
        if h < window - 1:
            total = total + product[h + 1, :, 2 * LANES :]
        two.append(jnp.maximum(total, 0.0))
    taps = jnp.concatenate([row_taps(plane) for plane in two], axis=0).astype(jnp.bfloat16)
    three = jnp.dot(taps, band_two[...], preferred_element_type=jnp.float32)
    three = three.reshape(window, high, LANES)[:, :rows]
    out_ref[...] = jnp.maximum(three, 0.0).astype(out_ref.dtype)


def local_call(kernel, out_shape, *operands):
    vmem = pl.BlockSpec(memory_space=pltpu.VMEM)
    return pl.pallas_call(
        kernel,
        out_shape=out_shape,
        in_specs=[vmem] * len(operands),
        out_specs=jax.tree.map(lambda _: vmem, out_shape),
        compiler_params=pltpu.CompilerParams(vmem_limit_bytes=8 << 20),
    )(*operands)


def filter_all(near, far, matrices, entries, groups, window, rows):
    *far, last = far
    planes = 3 * window
    width = near[0].shape[1]
    volume = local_call(
        functools.partial(volume_kernel, entries, groups, window),
        [
            jax.ShapeDtypeStruct((planes * rows, LANES), jnp.bfloat16),
            jax.ShapeDtypeStruct((planes * TILE, LANES), jnp.float32),
            jax.ShapeDtypeStruct(
                (planes_padded(planes, LANES // groups) * groups, width), jnp.bfloat16
            ),
        ],
        *near,
        *far,
    )
    return local_call(
        functools.partial(filter_kernel, entries, groups, window),
        jax.ShapeDtypeStruct((window, rows, LANES), jnp.bfloat16),
        *volume,
        last,
        *matrices,
    )


def fast_local(
    source_features,
    target_features,
    source_rows,
    target_cols,
    target_kernel_one,
    source_kernel,
    target_kernel_two,
):
    groups = source_kernel.shape[2]
    window = source_rows.shape[0]
    rows = target_features.shape[0]
    count = lax.axis_size("src")
    entries = entries_of(count)

    def exchange(block, mask):
        pairs = [(2 * s + t, 2 * (s ^ mask[t]) + 1 - t) for s in range(count) for t in range(2)]
        return lax.ppermute(block, ("src", "tgt"), pairs)

    early, last = rounds_of(count)
    ((mask, _),) = early
    held = pack(source_rows, source_features[:, 0], target_features[:, 0])
    arrived = exchange(held, (mask, mask))
    matrices = weights(
        target_cols,
        (target_kernel_one, source_kernel, target_kernel_two),
        [offsets for _, _, _, offsets, _ in entries],
    )
    arrived, matrices = lax.optimization_barrier((arrived, matrices))
    lines = jnp.concatenate([block[rows : rows + window] for block in (held, arrived)], axis=0)
    blank = jnp.zeros((whole_tiles(lines.shape[0]) - lines.shape[0], lines.shape[1]), lines.dtype)
    held = jnp.concatenate([held[:rows], arrived[:rows], lines, blank], axis=0)
    near = [held, *(exchange(held, mask) for mask in last)]
    far = [exchange(part, (0, 0)) for part in near]
    return filter_all(near, far, matrices, entries, groups, window, rows)[:, None]


def with_halo(block, sides, width):
    for axis, dim in sides:
        count = lax.axis_size(axis)
        forward = [(i, i + 1) for i in range(count - 1)]
        backward = [(target, source) for source, target in forward]
        low = lax.ppermute(
            lax.slice_in_dim(block, block.shape[dim] - width, None, axis=dim), axis, forward
        )
        high = lax.ppermute(lax.slice_in_dim(block, 0, width, axis=dim), axis, backward)
        block = jnp.concatenate([low, block, high], axis=dim)
    return block


def build_toeplitz(kernel, breadth):
    groups = kernel.shape[2]
    span_width = breadth * groups
    row_index = lax.broadcasted_iota(jnp.int32, (3, breadth, breadth), 1)
    col_index = lax.broadcasted_iota(jnp.int32, (3, breadth, breadth), 2)
    tap_index = lax.broadcasted_iota(jnp.int32, (3, breadth, breadth), 0)
    shifts = (row_index - col_index == tap_index - 1).astype(jnp.bfloat16)
    matrices = []
    for offset_y in range(3):
        banded = jnp.einsum(
            "xab,xio->aibo", shifts, kernel[offset_y], preferred_element_type=jnp.float32
        )
        matrices.append(banded.astype(jnp.bfloat16).reshape(span_width, span_width))
    return jnp.stack(matrices)


def banded_pass(slices, matrices):
    span_width = matrices.shape[1]
    running = jnp.dot(
        slices[0].reshape(-1, span_width), matrices[0], preferred_element_type=jnp.float32
    )
    for offset in range(1, 3):
        running = running + jnp.dot(
            slices[offset].reshape(-1, span_width),
            matrices[offset],
            preferred_element_type=jnp.float32,
        )
    return jnp.maximum(running, 0.0).astype(jnp.bfloat16).reshape(slices[0].shape)


def target_pass(padded, matrices):
    row_count = padded.shape[1] - 2
    return banded_pass([padded[:, offset : offset + row_count] for offset in range(3)], matrices)


def column_filter(neighbours, source_kernel, groups, window_rows):
    bordered = jnp.pad(neighbours, ((0, 0), (1, 1), (0, 0), (0, 0)))
    span_width = neighbours.shape[3]
    repeats = math.gcd(span_width // groups, max(1, 128 // groups))
    block_width = repeats * groups
    diagonal = jnp.einsum(
        "ab,yxij->yxaibj", jnp.eye(repeats, dtype=jnp.float32), source_kernel.astype(jnp.float32)
    )
    diagonal = diagonal.reshape(3, 3, block_width, block_width).astype(jnp.bfloat16)
    running = jnp.zeros((neighbours[1].size // block_width, block_width), jnp.float32)
    for offset in range(3):
        window = bordered[:, offset : offset + window_rows].reshape(3, -1, block_width)
        running = running + jnp.einsum(
            "xmc,xcd->md", window, diagonal[offset], preferred_element_type=jnp.float32
        )
    return jnp.maximum(running, 0.0).astype(jnp.bfloat16).reshape(neighbours[1].shape)


def local(
    source_features,
    target_features,
    source_rows,
    target_cols,
    target_kernel_one,
    source_kernel,
    target_kernel_two,
):
    groups = source_kernel.shape[2]
    channels = source_features.shape[2] // groups
    window_rows = source_rows.shape[0]
    selected = jnp.take(source_features[:, 0], source_rows, axis=0)
    columns = selected[None]
    column_count = columns.shape[0]
    columns = columns.reshape(column_count, window_rows, groups, channels)
    gathered = lax.all_gather(target_features, "src", axis=1, tiled=True)
    gathered = jnp.take(gathered, target_cols, axis=1)
    target_rows = gathered.shape[0]
    breadth = gathered.shape[1]
    grouped = gathered.reshape(target_rows, breadth, groups, channels)
    volume = jnp.einsum("khgc,rwgc->khrwg", columns, grouped, preferred_element_type=jnp.float32)
    volume = (
        (volume * channels ** (-0.5))
        .astype(jnp.bfloat16)
        .reshape(column_count * window_rows, target_rows, breadth * groups)
    )
    padded = with_halo(volume, (("tgt", 1),), 1)
    filtered_one = target_pass(padded, build_toeplitz(target_kernel_one, breadth))
    neighbours = with_halo(filtered_one[None], (("src", 0),), 1)
    filtered_two = column_filter(neighbours, source_kernel, groups, window_rows)
    padded_last = with_halo(filtered_two, (("tgt", 1),), 1)
    filtered_three = target_pass(padded_last, build_toeplitz(target_kernel_two, breadth))
    return filtered_three[:, None]


def solution(mesh):
    def step(*args):
        source, target, source_rows, cols, _, source_kernel, _ = args
        count = lax.axis_size("src")
        fits = (
            lax.axis_size("tgt") == 2
            and count == 8
            and source.shape[1] == 1
            and target.shape[1] == 1
            and cols.shape[0] == count
            and count * source_kernel.shape[2] == LANES
            and source_rows.shape[0] <= TILE
            and target.shape[0] % (2 * TILE) == 0
        )
        return (fast_local if fits else local)(*args)

    return jax.shard_map(
        step,
        mesh=mesh,
        in_specs=(
            P("pair", "src", None),
            P(("pair", "tgt"), "src", None),
            P("pair"),
            P("pair"),
            P(),
            P(),
            P(),
        ),
        out_specs=P("pair", "src", "tgt", None),
        check_vma=False,
    )
```
